32 devices in a mesh: gx: 2 (over y), gy: 4 (over z), gz: 4 (over x, core).
Axes of the slice: x: 2, y: 2, z: 4, core: 2. Of those that a mesh axis runs over, the one named last changes fastest.
Arguments:
- gas_temp: float32 [128, 128, 1024], P('gz', 'gx', 'gy'), may hold values from 1 to 8
- fuel_frac: float32 [128, 128, 1024], P('gz', 'gx', 'gy'), may hold values from 0 to 1
- velocity: float32 [3, 128, 128, 1024], P(None, 'gz', 'gx', 'gy'), may hold values from -3 to 3
- wall_flags: int32 [128, 1024], P('gx', 'gy'), may hold values 0 or 1
- solid_temp: float32 [64, 256, 2048], P(None, ('gx', 'gy'), 'gz'), may hold values from 1 to 3
- diffusivity: float32 [64, 256, 2048], P(None, ('gx', 'gy'), 'gz'), may hold values from 0.03 to 0.15
- gas_owner: int32 [256, 2048], P(('gx', 'gy'), 'gz'), may hold values from 0 to 131071, as said below
Outputs:
- gas_temp_new: float32 [128, 128, 1024], P('gz', 'gx', 'gy')
- fuel_frac_new: float32 [128, 128, 1024], P('gz', 'gx', 'gy')
- solid_temp_new: float32 [64, 256, 2048], P(None, ('gx', 'gy'), 'gz')
The draws below stay inside these ranges and needn't reach their ends.
Inputs may be any that keep to these rules, and one draw needn't show every extreme that they name: gas_owner[p, q] = a * 1024 + b where a differs from p // 2 by at most 4 modulo 128 and b differs from q // 2 by at most 4 modulo 1024; both offsets reach 4 in both directions.
All inputs are finite; a program needn't handle non-finite values. No bound on the sum of `wall_flags` on one device may be relied on, other than what follows from the above.
Results may differ from the reference program's by a relative error of at most 0.00002.
Values sent between devices are 32-bit elements; how exact they have to be, the bound alone decides.
A program may use at most 128 MiB of HBM per device.

```python
import math
import jax
import jax.numpy as jnp

SZ = 64
SUBSTEPS = 4
DISP = 4
NX = 128
NY = 1024
NZ = 128
SX = 256
SY = 2048


def draw_gas_owner(key, part):
    key_rows = jax.random.fold_in(key, 11)
    key_cols = jax.random.fold_in(key, 23)
    shift_rows = jax.random.randint(key_rows, (SX, SY), -DISP, DISP + 1)
    shift_cols = jax.random.randint(key_cols, (SX, SY), -DISP, DISP + 1)
    base_rows = jnp.arange(SX, dtype=jnp.int32)[:, None] // 2
    base_cols = jnp.arange(SY, dtype=jnp.int32)[None, :] // 2
    gas_row = (base_rows + shift_rows) % NX
    gas_col = (base_cols + shift_cols) % NY
    return (gas_row * NY + gas_col).astype(jnp.int32)


def touch_ends(entries, own_key, least, high):
    extent = entries.shape
    spot = [jax.random.randint(jax.random.fold_in(own_key, axis), (), 0, extent[axis]) for axis in range(len(extent))]
    entries = entries.at[tuple(spot)].set(least)
    longest = extent.index(max(extent))
    spot[longest] = (spot[longest] + 1) % extent[longest]
    return entries.at[tuple(spot)].set(high)


def shard_levels(key, extent, pieces, low, largest):
    def one(dim, parts):
        draws = jax.random.uniform(jax.random.fold_in(jax.random.fold_in(key, 6), dim), (parts,), jnp.float32, low / len(pieces), largest / len(pieces))
        return jnp.repeat(jnp.exp(draws), extent[dim] // parts).reshape((-1,) + (1,) * (len(extent) - dim - 1))

    factor_of = one(*pieces[0])
    for cut in pieces[1:]:
        factor_of = factor_of * one(*cut)
    return factor_of


def centred(own_key, shape, spread, bound, split=(), kind=jnp.bfloat16):
    array = jax.random.normal(own_key, shape, jnp.float32) * spread
    if len(split) > 0:
        array = shard_levels(own_key, shape, split, -0.22, 0.18) * array
    return jnp.clip(array, min=-bound, max=bound).astype(kind)


def setup_inputs(seed: int = 0) -> dict:
    keys = jax.random.split(jax.random.key(seed), 8)
    return {
        "gas_temp": jnp.clip(1.0 + 7.0 * jax.random.uniform(keys[0], (NZ, NX, NY), jnp.float32) ** shard_levels(keys[0], (NZ, NX, NY), ((0, 4), (1, 2), (2, 4)), -0.2, 0.2), 1.0, 8.0),
        "fuel_frac": jnp.clip(1.0 * jax.random.uniform(keys[1], (NZ, NX, NY), jnp.float32) ** shard_levels(keys[1], (NZ, NX, NY), ((0, 4), (1, 2), (2, 4)), -0.2, 0.2), 0.0, 1.0),
        "velocity": centred(keys[2], (3, NZ, NX, NY), 0.5, 3.0, ((1, 4), (2, 2), (3, 4)), jnp.float32),
        "wall_flags": touch_ends((jax.random.randint(keys[3], (NX, NY), 0, 4) < 3).astype(jnp.int32), jax.random.fold_in(keys[3], 1), 0, 1),
        "solid_temp": jnp.clip(1.0 + 2.0 * jax.random.uniform(keys[4], (SZ, SX, SY), jnp.float32) ** shard_levels(keys[4], (SZ, SX, SY), ((1, 8), (2, 4)), -0.2, 0.2), 1.0, 3.0),
        "diffusivity": jnp.clip(jnp.exp(math.log(0.15) - 1.609438 * jax.random.uniform(keys[5], (SZ, SX, SY), jnp.float32) ** shard_levels(keys[5], (SZ, SX, SY), ((1, 8), (2, 4)), -0.2, 0.2)), 0.03, 0.15),
        "gas_owner": draw_gas_owner(jax.random.fold_in(keys[7], 71), 0),
    }


FILM_COEF = 0.15
SOURCE_GAIN = 0.25
COOLANT = 1.0
DIFFUSE_TEMP = 0.2
DIFFUSE_FUEL = 0.15
TIME_STEP = 0.2
RATE_CONST = 1.0
ACTIVATION = 4.0
HEAT_RELEASE = 3.0


def gas_update(fields, z_below, z_above, x_below, x_above, y_below, y_above, velocity):
    advect = 0.5 * (velocity[0] * (z_above - z_below) + velocity[1] * (x_above - x_below) + velocity[2] * (y_above - y_below))
    nearby = z_below + z_above + x_below + x_above + y_below + y_above
    reaction = RATE_CONST * fields[1] * jnp.exp(-ACTIVATION / fields[0])
    temp_new = fields[0] + TIME_STEP * (-advect[0] + DIFFUSE_TEMP * (nearby[0] - 6.0 * fields[0]) + HEAT_RELEASE * reaction)
    fuel_new = fields[1] + TIME_STEP * (-advect[1] + DIFFUSE_FUEL * (nearby[1] - 6.0 * fields[1]) - reaction)
    return temp_new, fuel_new


def solid_step(solid_now, diffusivity, wall_flux):
    bottom_ghost = jnp.full_like(solid_now[:1], COOLANT)
    z_below = jnp.concatenate([solid_now[:1], solid_now[:-1]], 0)
    z_above = jnp.concatenate([solid_now[1:], bottom_ghost], 0)
    nearby = z_below + z_above + jnp.roll(solid_now, 1, 1) + jnp.roll(solid_now, -1, 1)
    nearby = nearby + jnp.roll(solid_now, 1, 2) + jnp.roll(solid_now, -1, 2)
    solid_next = solid_now + diffusivity * (nearby - 6.0 * solid_now)
    return solid_next.at[0].add(SOURCE_GAIN * wall_flux)


def reference(gas_temp, fuel_frac, velocity, wall_flags, solid_temp, diffusivity, gas_owner):
    gas_face = gas_temp[0]
    film = FILM_COEF * wall_flags.astype(jnp.float32) * gas_face ** 0.7
    gas_at = gas_face.reshape(-1)[gas_owner]
    film_at = film.reshape(-1)[gas_owner]
    wall_flux = film_at * (gas_at - solid_temp[0])
    solid_now = solid_temp
    for substep in range(SUBSTEPS):
        solid_now = solid_step(solid_now, diffusivity, wall_flux)
    surface = solid_now[0]
    wall_temp = 0.25 * surface.reshape(NX, 2, NY, 2).sum(axis=(1, 3))
    fields = jnp.stack([gas_temp, fuel_frac])
    low_temp = jnp.where(wall_flags == 1, 2.0 * wall_temp - gas_temp[0], gas_temp[0])
    low_layer = jnp.stack([low_temp, fuel_frac[0]])
    z_below = jnp.concatenate([low_layer[:, None], fields[:, :-1]], 1)
    z_above = jnp.concatenate([fields[:, 1:], fields[:, -1:]], 1)
    temp_new, fuel_new = gas_update(fields, z_below, z_above,
                                    jnp.roll(fields, 1, 2), jnp.roll(fields, -1, 2),
                                    jnp.roll(fields, 1, 3), jnp.roll(fields, -1, 3), velocity)
    return temp_new, fuel_new, solid_now
```

```python
import functools

import jax
import jax.numpy as jnp
from jax import lax
from jax.experimental import pallas as pl
from jax.experimental.pallas import tpu as pltpu
from jax.sharding import PartitionSpec as P

SUBSTEPS = 4
DISP = 4

FILM_COEF = 0.15
SOURCE_GAIN = 0.25
COOLANT = 1.0
DIFFUSE_TEMP = 0.2
DIFFUSE_FUEL = 0.15
TIME_STEP = 0.2
RATE_CONST = 1.0
ACTIVATION = 4.0
HEAT_RELEASE = 3.0

LANES = 128
HALO = SUBSTEPS
REACH = DISP + HALO // 2
SPAN = 2 * DISP + 1
HIGHEST = lax.Precision.HIGHEST
VMEM = pl.BlockSpec(memory_space=pltpu.VMEM)


def iota(shape, dim):
    return lax.broadcasted_iota(jnp.int32, shape, dim)


def shift_pairs(count):
    forward = [(i, (i + 1) % count) for i in range(count)]
    return forward, [(b, a) for a, b in forward]


def exchange(first, last, axis):
    forward, backward = shift_pairs(lax.axis_size(axis))
    return lax.ppermute(first, axis, backward), lax.ppermute(last, axis, forward)


def pack_kernel(temp_lo, temp_hi, fuel_lo, fuel_hi, s_lo, s_hi, d_lo, d_hi, c_lo, c_hi, gas_out, wall_out):
    nz, rows, _ = temp_lo.shape
    layers, wrows, _ = s_lo.shape
    per = LANES // HALO
    lane = iota((rows, LANES), 1)

    def gas_body(z, acc):
        low, high = acc
        for f, (lo, hi) in enumerate(((temp_lo, temp_hi), (fuel_lo, fuel_hi))):
            k = f * nz + z
            low = jnp.where(lane == k, pltpu.roll(lo[z], k, 1), low)
            high = jnp.where(lane == k, pltpu.roll(hi[z], k + 1, 1), high)
        return low, high

    zero = jnp.zeros((rows, LANES), jnp.float32)
    low, high = lax.fori_loop(0, nz, gas_body, (zero, zero))
    gas_out[0] = low
    gas_out[1] = high

    group_of = iota((wrows, LANES), 1) // HALO
    groups = layers // per
    wzero = jnp.zeros((wrows, LANES), jnp.float32)
    for g in range(groups):

        def wall_body(k, acc):
            out = []
            for n, ref in enumerate((s_lo, s_hi, d_lo, d_hi)):
                shift = HALO * k if n % 2 == 0 else lax.rem(HALO * k + HALO, LANES)
                out.append(jnp.where(group_of == k, pltpu.roll(ref[g * per + k], shift, 1), acc[n]))
            return tuple(out)

        packed = lax.fori_loop(0, per, wall_body, (wzero,) * 4)
        wall_out[0, g] = packed[0]
        wall_out[1, g] = packed[1]
        wall_out[0, groups + g] = packed[2]
        wall_out[1, groups + g] = packed[3]
    wall_out[0, 2 * groups] = c_lo[...]
    wall_out[1, 2 * groups] = pltpu.roll(c_hi[...], HALO, 1)


def gas_kernel(step_layers, temp, fuel, vel, x_low, x_high, y_low, y_high, z_low, z_high, temp_out, fuel_out):
    nz, rows, cols = temp.shape
    base = pl.program_id(0) * step_layers
    row = iota((rows, cols), 0)
    col = iota((rows, cols), 1)
    tiles = cols // LANES

    def wide(x):
        return jnp.concatenate([x] * tiles, axis=1)

    for i in range(step_layers):
        z = base + i
        centers = (temp[z], fuel[z])
        reaction = RATE_CONST * centers[1] * jnp.exp(-ACTIVATION / centers[0])
        for f, ref in enumerate((temp, fuel)):
            c = centers[f]
            if i == 0:
                below = jnp.where(z == 0, z_low[f], ref[jnp.maximum(z - 1, 0)])
            else:
                below = ref[z - 1]
            if i == step_layers - 1:
                above = jnp.where(z == nz - 1, z_high[f], ref[jnp.minimum(z + 1, nz - 1)])
            else:
                above = ref[z + 1]
            xl = jnp.where(row == 0, x_low[f, pl.ds(z, 1), :], pltpu.roll(c, 1, 0))
            xh = jnp.where(row == rows - 1, x_high[f, pl.ds(z, 1), :], pltpu.roll(c, rows - 1, 0))
            k = f * nz + z
            edge_l = wide(pltpu.roll(y_low[...], LANES - k, 1))
            edge_h = wide(pltpu.roll(y_high[...], LANES - 1 - k, 1))
            yl = jnp.where(col == 0, edge_l, pltpu.roll(c, 1, 1))
            yh = jnp.where(col == cols - 1, edge_h, pltpu.roll(c, cols - 1, 1))
            advect = 0.5 * (vel[0, i] * (above - below) + vel[1, i] * (xh - xl) + vel[2, i] * (yh - yl))
            nearby = below + above + xl + xh + yl + yh
            if f == 0:
                rate = -advect + DIFFUSE_TEMP * (nearby - 6.0 * c) + HEAT_RELEASE * reaction
                temp_out[i] = c + TIME_STEP * rate
            else:
                rate = -advect + DIFFUSE_FUEL * (nearby - 6.0 * c) - reaction
                fuel_out[i] = c + TIME_STEP * rate


def wall_kernel(s, d, code, after, before, packs, face, s_out, tile_out, a, b, dd, code_s, gas_s, film_s, up_s, flux_s):
    layers, rows, cols = s.shape
    ext_r, ext_c = a.shape[1:]
    up_r = up_s.shape[1]
    per = LANES // HALO
    groups = layers // per
    lane = iota((ext_r, LANES), 1)

    def fill(dst, z, src, layer, group, k):
        dst[z, 0:rows, 0:cols] = src[z]
        dst[z, rows : rows + HALO, 0:cols] = after[layer]
        dst[z, rows + HALO : rows + 2 * HALO, 0:cols] = before[layer]
        right = pltpu.roll(packs[0, group], LANES - HALO * k, 1)
        left = pltpu.roll(packs[1, group], LANES - HALO - HALO * k, 1)
        dst[z, :, cols:] = jnp.where(lane < LANES // 2, right, left)

    for g in range(groups):

        def fill_body(k, carry):
            z = g * per + k
            fill(a, z, s, z, g, k)
            fill(dd, z, d, layers + z, groups + g, k)
            return carry

        lax.fori_loop(0, per, fill_body, 0)
    a[layers] = jnp.full((ext_r, ext_c), COOLANT, jnp.float32)
    b[layers] = jnp.full((ext_r, ext_c), COOLANT, jnp.float32)

    code_s[...] = jnp.full((up_r, ext_c), -1.0, jnp.float32)
    code_s[0:rows, 0:cols] = code[...]
    code_s[rows : rows + HALO, 0:cols] = after[2 * layers]
    code_s[up_r - HALO : up_r, 0:cols] = before[2 * layers]
    right = packs[0, 2 * groups]
    left = pltpu.roll(packs[1, 2 * groups], LANES - HALO, 1)
    edge = jnp.where(lane < LANES // 2, right, left)
    code_s[0:rows, cols:] = edge[0:rows]
    code_s[rows : rows + HALO, cols:] = edge[rows : rows + HALO]
    code_s[up_r - HALO : up_r, cols:] = edge[rows + HALO :]

    fr, fc = face.shape[1:]
    up_rows = (iota((up_r, fr), 0) // 2 == iota((up_r, fr), 1)).astype(jnp.float32)
    up_cols = (iota((fc, ext_c), 0) == iota((fc, ext_c), 1) // 2).astype(jnp.float32)
    for n in range(2):
        tall = jnp.dot(up_rows, face[n], precision=HIGHEST, preferred_element_type=jnp.float32)
        up_s[n] = jnp.dot(tall, up_cols, precision=HIGHEST, preferred_element_type=jnp.float32)
    gas_s[...] = jnp.zeros((up_r, ext_c), jnp.float32)
    film_s[...] = jnp.zeros((up_r, ext_c), jnp.float32)

    def pick_body(j, carry):
        shift = lax.rem(ext_c + 2 * DISP - 2 * j, ext_c)
        gas_w = pltpu.roll(up_s[0], shift, 1)
        film_w = pltpu.roll(up_s[1], shift, 1)
        for r in range(SPAN):
            down = (2 * DISP - 2 * r) % up_r
            hit = code_s[...] == (r * SPAN + j).astype(jnp.float32)
            gas_s[...] = jnp.where(hit, pltpu.roll(gas_w, down, 0) if down else gas_w, gas_s[...])
            film_s[...] = jnp.where(hit, pltpu.roll(film_w, down, 0) if down else film_w, film_s[...])
        return carry

    lax.fori_loop(0, SPAN, pick_body, 0)

    surf = a[0]
    flux_s[0:rows] = film_s[0:rows] * (gas_s[0:rows] - surf[0:rows])
    half = rows + HALO
    flux_s[rows:half] = film_s[rows:half] * (gas_s[rows:half] - surf[rows:half])
    tail = slice(up_r - HALO, up_r)
    flux_s[half:] = film_s[tail] * (gas_s[tail] - surf[half:])

    bufs = (a, b)
    for step in range(SUBSTEPS):
        src, dst = bufs[step % 2], bufs[(step + 1) % 2]
        last = step == SUBSTEPS - 1

        def body(z, carry, src=src, dst=dst, last=last):
            if last:
                full = src[z]
                c = full[0:rows]
                below = src[jnp.maximum(z - 1, 0), 0:rows, :]
                above = src[z + 1, 0:rows, :]
                coef = dd[z, 0:rows, :]
            else:
                full = c = src[z]
                below = src[jnp.maximum(z - 1, 0)]
                above = src[z + 1]
                coef = dd[z]
            n = c.shape[0]
            nearby = below + above + pltpu.roll(full, 1, 0)[0:n] + pltpu.roll(full, ext_r - 1, 0)[0:n]
            nearby = nearby + pltpu.roll(c, 1, 1) + pltpu.roll(c, ext_c - 1, 1)
            out = c + coef * (nearby - 6.0 * c)
            if last:
                s_out[z] = out[:, 0:cols]
            else:
                dst[z] = out
            return carry

        lax.fori_loop(0, layers, body, 0)
        if last:
            s_out[0] = s_out[0] + SOURCE_GAIN * flux_s[0:rows, 0:cols]
        else:
            dst[0] = dst[0] + SOURCE_GAIN * flux_s[...]

    hr, hc = rows // 2, cols // 2
    fold_r = 0.5 * (iota((hr, rows), 0) == iota((hr, rows), 1) // 2).astype(jnp.float32)
    fold_c = 0.5 * (iota((cols, hc), 0) // 2 == iota((cols, hc), 1)).astype(jnp.float32)
    short = jnp.dot(fold_r, s_out[0], precision=HIGHEST, preferred_element_type=jnp.float32)
    tile_out[...] = jnp.dot(short, fold_c, precision=HIGHEST, preferred_element_type=jnp.float32)


def shards(gas_temp, fuel_frac, velocity, wall_flags, solid_temp, diffusivity, gas_owner):
    nx, ny, nz = lax.axis_size("gx"), lax.axis_size("gy"), lax.axis_size("gz")
    gx, gy, gz = lax.axis_index("gx"), lax.axis_index("gy"), lax.axis_index("gz")
    assert ny == nz
    layers_g, rows_g, cols_g = gas_temp.shape
    layers, rows, cols = solid_temp.shape
    assert cols == 2 * cols_g and rows * ny == 2 * rows_g and 2 * layers_g <= LANES
    strip = rows // 2
    everywhere = ("gx", "gy", "gz")

    def rank(i, j, k):
        return (i * ny + j) * nz + k

    gas_face = gas_temp[0]
    film = FILM_COEF * wall_flags.astype(jnp.float32) * gas_face**0.7
    pair = jnp.stack([gas_face, film])
    after, before = exchange(pair[:, :8], pair[:, -8:], "gx")
    pair = jnp.concatenate([before, pair, after], axis=1)
    side = 32
    after, before = exchange(pair[:, :, :side], pair[:, :, -side:], "gy")
    ext_c = cols + LANES
    ext_half = ext_c // 2
    pair = jnp.concatenate([pair, after, before], axis=2)
    assert pair.shape[2] == ext_half
    pair = jnp.pad(pair, ((0, 0), (0, 0), (0, -ext_half % LANES)))

    all_cols = cols_g * ny
    all_rows = rows_g * nx
    p = (gx * ny + gy) * strip + iota((rows, cols), 0) // 2
    q = gz * cols_g + iota((rows, cols), 1) // 2
    down = (gas_owner // all_cols - p + DISP + all_rows) % all_rows
    along = (gas_owner % all_cols - q + DISP + all_cols) % all_cols
    code = (down * SPAN + along).astype(jnp.float32)

    last_g = cols_g // LANES - 1
    last_w = cols // LANES - 1
    groups = 2 * (layers // (LANES // HALO)) + 1

    def lane_tile(lead, index):
        shape = tuple(lead) + (LANES,)
        return pl.BlockSpec(shape, lambda i: (0,) * len(lead) + (index,))

    gas_lead, wall_lead = (layers_g, rows_g), (layers, rows)
    gas_edges, wall_edges = pl.pallas_call(
        pack_kernel,
        grid=(1,),
        out_shape=(
            jax.ShapeDtypeStruct((2, rows_g, LANES), jnp.float32),
            jax.ShapeDtypeStruct((2, groups, rows, LANES), jnp.float32),
        ),
        in_specs=[
            lane_tile(gas_lead, 0),
            lane_tile(gas_lead, last_g),
            lane_tile(gas_lead, 0),
            lane_tile(gas_lead, last_g),
            lane_tile(wall_lead, 0),
            lane_tile(wall_lead, last_w),
            lane_tile(wall_lead, 0),
            lane_tile(wall_lead, last_w),
            lane_tile((rows,), 0),
            lane_tile((rows,), last_w),
        ],
        compiler_params=pltpu.CompilerParams(vmem_limit_bytes=32 << 20),
        cost_estimate=pl.CostEstimate(flops=4_000_000, bytes_accessed=8 << 20, transcendentals=0),
        name="pack",
    )(gas_temp, gas_temp, fuel_frac, fuel_frac, solid_temp, solid_temp, diffusivity, diffusivity, code, code)

    y_high, y_low = exchange(gas_edges[0], gas_edges[1], "gy")
    x_high, x_low = exchange(
        jnp.stack([gas_temp[:, 0], fuel_frac[:, 0]]), jnp.stack([gas_temp[:, -1], fuel_frac[:, -1]]), "gx"
    )
    first = jnp.stack([gas_temp[0], fuel_frac[0]])
    final = jnp.stack([gas_temp[-1], fuel_frac[-1]])
    z_high, z_low = exchange(first, final, "gz")
    z_low = jnp.where(gz == 0, first, z_low)
    z_high = jnp.where(gz == nz - 1, final, z_high)

    line = ("gx", "gy")

    def edge_rows(cut):
        return jnp.concatenate([solid_temp[:, cut], diffusivity[:, cut], code[None, cut]], axis=0)

    rows_first, rows_last, y_low, y_high, pair = lax.optimization_barrier(
        (edge_rows(slice(0, HALO)), edge_rows(slice(rows - HALO, rows)), y_low, y_high, pair)
    )
    rows_after, rows_before = exchange(rows_first, rows_last, line)
    side_after, side_before = exchange(wall_edges[0], wall_edges[1], "gz")
    sides = jnp.stack([side_after, side_before])

    step_layers = 4
    block = (step_layers, rows_g, cols_g)
    temp_new, fuel_new = pl.pallas_call(
        functools.partial(gas_kernel, step_layers),
        grid=(layers_g // step_layers,),
        out_shape=(jax.ShapeDtypeStruct(gas_temp.shape, jnp.float32),) * 2,
        in_specs=[VMEM, VMEM, pl.BlockSpec((3,) + block, lambda i: (0, i, 0, 0))] + [VMEM] * 6,
        out_specs=(pl.BlockSpec(block, lambda i: (i, 0, 0)),) * 2,
        compiler_params=pltpu.CompilerParams(vmem_limit_bytes=32 << 20),
        cost_estimate=pl.CostEstimate(flops=60_000_000, bytes_accessed=24 << 20, transcendentals=1 << 19),
        name="gas",
    )(gas_temp, fuel_frac, velocity, x_low, x_high, y_low, y_high, z_low, z_high)

    sides, pair, temp_new = lax.optimization_barrier((sides, pair, temp_new))
    pad_rows = -(strip + 2 * REACH) % 8
    face = None
    for j in range(ny):
        top = 8 + j * strip
        band = jnp.concatenate(
            [
                pair[:, top : top + strip + REACH],
                pair[:, top - REACH : top],
                jnp.zeros((2, pad_rows, pair.shape[2]), jnp.float32),
            ],
            axis=1,
        )
        pairs = [(rank(i, k, 0), rank(i, j, k)) for i in range(nx) for k in range(ny)]
        got = lax.ppermute(band, everywhere, pairs)
        face = got if face is None else face + got

    corner_after, corner_before = exchange(sides[:, :, :HALO], sides[:, :, -HALO:], line)
    packs = jnp.concatenate([sides, corner_after, corner_before], axis=2)

    ext_r = rows + 2 * HALO
    up_r = rows + 4 * REACH
    ext = pltpu.VMEM((layers + 1, ext_r, ext_c), jnp.float32)
    up = pltpu.VMEM((up_r, ext_c), jnp.float32)
    solid_new, tile = pl.pallas_call(
        wall_kernel,
        out_shape=(
            jax.ShapeDtypeStruct(solid_temp.shape, jnp.float32),
            jax.ShapeDtypeStruct((strip, cols_g), jnp.float32),
        ),
        in_specs=[VMEM] * 7,
        out_specs=(VMEM, VMEM),
        scratch_shapes=[
            ext,
            ext,
            ext,
            up,
            up,
            up,
            pltpu.VMEM((2, up_r, ext_c), jnp.float32),
            pltpu.VMEM((ext_r, ext_c), jnp.float32),
        ],
        compiler_params=pltpu.CompilerParams(vmem_limit_bytes=58 << 20),
        cost_estimate=pl.CostEstimate(flops=120_000_000, bytes_accessed=40 << 20, transcendentals=0),
        name="wall",
    )(solid_temp, diffusivity, code, rows_after, rows_before, packs, face)

    bands = []
    for j in range(ny):
        pairs = [(rank(i, j, k), rank(i, k, 0)) for i in range(nx) for k in range(ny)]
        bands.append(lax.ppermute(tile, everywhere, pairs))
    wall_temp = jnp.concatenate(bands, axis=0)
    coupled = (wall_flags == 1) & (gz == 0)
    gap = jnp.where(coupled, 2.0 * (wall_temp - gas_face), 0.0)
    wall_term = TIME_STEP * (0.5 * velocity[0, 0] + DIFFUSE_TEMP) * gap
    temp_new = temp_new.at[0].add(wall_term)
    return (temp_new, fuel_new, solid_new)


def solution(mesh):
    placed = (
        P("gz", "gx", "gy"),
        P("gz", "gx", "gy"),
        P(None, "gz", "gx", "gy"),
        P("gx", "gy"),
        P(None, ("gx", "gy"), "gz"),
        P(None, ("gx", "gy"), "gz"),
        P(("gx", "gy"), "gz"),
    )
    return jax.shard_map(
        shards,
        mesh=mesh,
        in_specs=placed,
        out_specs=(P("gz", "gx", "gy"), P("gz", "gx", "gy"), P(None, ("gx", "gy"), "gz")),
        check_vma=False,
    )
```
